32 devices in a mesh: gx: 4 (over z), gy: 2 (over core), gz: 4 (over y, x).
Axes of the slice: x: 2, y: 2, z: 4, core: 2. Of those that a mesh axis runs over, the one named last changes fastest.
Arguments:
- offsets: float32 [3, 8, 4, 8, 128], P(None, 'gx', 'gy', 'gz'), may hold values from 0 to 1
- velocities: float32 [3, 8, 4, 8, 128], P(None, 'gx', 'gy', 'gz'), may hold values from -3 to 3
- smoothing: float32 [8, 4, 8, 128], P('gx', 'gy', 'gz'), may hold values from 0.6 to 1
- mass: float32 [8, 4, 8, 128], P('gx', 'gy', 'gz'), may hold values from 0.004 to 0.016
- entropy: float32 [8, 4, 8, 128], P('gx', 'gy', 'gz'), may hold values from 0.5 to 2
- prior_density: float32 [8, 4, 8, 128], P('gx', 'gy', 'gz'), may hold values from 0.5 to 2
- active: int32 [8, 4, 8, 128], P('gx', 'gy', 'gz'), may hold values from 0 to 1, as said below
Outputs:
- density: float32 [8, 4, 8, 128], P('gx', 'gy', 'gz')
- acceleration: float32 [3, 8, 4, 8, 128], P(None, 'gx', 'gy', 'gz')
The draws below stay inside these ranges and needn't reach their ends.
Inputs may be any that keep to these rules, and one draw needn't show every extreme that they name: 1 marks an active particle; activity is set in aligned blocks of 2 x 2 x 2 cells, and some blocks hold no active particle.
All inputs are finite; a program needn't handle non-finite values.
Results may differ from the reference program's by a relative error of at most 0.0001.
Values sent between devices are 32-bit elements; how exact they have to be, the bound alone decides.
No kernel may reach another device: no remote copies, remote signals or barrier semaphores. Data moves between devices by JAX's collectives and lax.ppermute only.
A program may use at most 64 MiB of HBM per device.

```python
import math
import jax
import jax.numpy as jnp
from jax import lax

P_SIZE = 128
NX = 8
NY = 4
NZ = 8


def draw_active(key, part):
    level_key, bit_key = jax.random.split(jax.random.fold_in(key, 11))
    levels = jax.random.randint(level_key, (NX // 2, NY // 2, NZ // 2), 0, 4)
    table = jnp.array([0, 0, 6, 26], dtype=jnp.int32)
    cutoff = table[levels]
    cutoff = jnp.repeat(jnp.repeat(jnp.repeat(cutoff, 2, axis=0), 2, axis=1), 2, axis=2)
    draws = jax.random.randint(bit_key, (NX, NY, NZ, P_SIZE), 0, 64)
    return (draws < cutoff[..., None]).astype(jnp.int32)


def block_levels(key, extent, pieces, smallest, high):
    level = 1.0
    for dim, blocks in pieces:
        steps = jax.random.uniform(jax.random.fold_in(jax.random.fold_in(key, 6), dim), (blocks,), jnp.float32, smallest / len(pieces), high / len(pieces))
        level = level * jnp.repeat(jnp.exp(steps), extent[dim] // blocks).reshape((-1,) + (1,) * (len(extent) - 1 - dim))
    return level


def scatter_about(stream_key, extent, spread, bound, cuts=(), kind=jnp.bfloat16):
    drawn = jax.random.normal(stream_key, extent, jnp.float32) * spread
    if len(cuts) > 0:
        drawn = block_levels(stream_key, extent, cuts, -0.22, 0.18) * drawn
    return jnp.clip(drawn, min=-bound, max=bound).astype(kind)


def setup_inputs(seed: int = 0) -> dict:
    seeds = jax.random.split(jax.random.key(seed), 8)
    offsets = jnp.clip(1.0 * jax.random.uniform(seeds[0], (3, NX, NY, NZ, P_SIZE), jnp.float32) ** block_levels(seeds[0], (3, NX, NY, NZ, P_SIZE), ((1, 4), (2, 2), (3, 4)), -0.2, 0.2), 0.0, 1.0)
    velocities = scatter_about(seeds[1], (3, NX, NY, NZ, P_SIZE), 0.5, 3.0, ((1, 4), (2, 2), (3, 4)), jnp.float32)
    smoothing = jnp.clip(jnp.exp(math.log(1.0) - 0.5108256 * jax.random.uniform(seeds[2], (NX, NY, NZ, P_SIZE), jnp.float32) ** block_levels(seeds[2], (NX, NY, NZ, P_SIZE), ((0, 4), (1, 2), (2, 4)), -0.2, 0.2)), 0.6, 1.0)
    mass = jnp.clip(jnp.exp(math.log(0.016) - 1.3862944 * jax.random.uniform(seeds[3], (NX, NY, NZ, P_SIZE), jnp.float32) ** block_levels(seeds[3], (NX, NY, NZ, P_SIZE), ((0, 4), (1, 2), (2, 4)), -0.2, 0.2)), 0.004, 0.016)
    entropy = jnp.clip(jnp.exp(math.log(2.0) - 1.3862944 * jax.random.uniform(seeds[4], (NX, NY, NZ, P_SIZE), jnp.float32) ** block_levels(seeds[4], (NX, NY, NZ, P_SIZE), ((0, 4), (1, 2), (2, 4)), -0.2, 0.2)), 0.5, 2.0)
    prior_density = jnp.clip(jnp.exp(math.log(2.0) - 1.3862944 * jax.random.uniform(seeds[5], (NX, NY, NZ, P_SIZE), jnp.float32) ** block_levels(seeds[5], (NX, NY, NZ, P_SIZE), ((0, 4), (1, 2), (2, 4)), -0.2, 0.2)), 0.5, 2.0)
    active = draw_active(jax.random.fold_in(seeds[7], 71), 0)
    return {"offsets": offsets, "velocities": velocities, "smoothing": smoothing, "mass": mass, "entropy": entropy, "prior_density": prior_density, "active": active}


kernel_norm = 21.0 / (2.0 * math.pi)
visc_alpha = 1.0
visc_beta = 2.0

def neighbour_shifts():
    return [(step_x, step_y, step_z) for step_x in (-1, 0, 1) for step_y in (-1, 0, 1) for step_z in (-1, 0, 1)]

def kernel_terms(radius_sq, smooth):
    ratio = jnp.sqrt(radius_sq) / smooth
    inside = jnp.maximum(1.0 - ratio, 0.0)
    value = kernel_norm / smooth ** 3 * inside ** 4 * (1.0 + 4.0 * ratio)
    slope = -20.0 * kernel_norm / smooth ** 5 * inside ** 3
    return (value, slope)

def neighbour_cells(around, shift, center):
    size_x, size_y, size_z = (center.shape[1], center.shape[2], center.shape[3])
    return around[:, 1 + shift[0]:1 + shift[0] + size_x, 1 + shift[1]:1 + shift[1] + size_y, 1 + shift[2]:1 + shift[2] + size_z]

def separation(center, neighbour, shift):
    return [center[axis_id][..., :, None] - neighbour[axis_id][..., None, :] - float(shift[axis_id]) for axis_id in range(3)]

def density_block(around):
    center = around[:, 1:-1, 1:-1, 1:-1]
    smooth = center[6][..., :, None]
    total = jnp.zeros(center.shape[1:], jnp.float32)
    for shift in neighbour_shifts():
        neighbour = neighbour_cells(around, shift, center)
        parts = separation(center, neighbour, shift)
        radius_sq = parts[0] ** 2 + parts[1] ** 2 + parts[2] ** 2
        value, slope = kernel_terms(radius_sq, smooth)
        total = total + lax.optimization_barrier(jnp.sum(neighbour[7][..., None, :] * value, axis=-1))
    return total

def force_block(around):
    center = around[:, 1:-1, 1:-1, 1:-1]
    smooth_own = center[6][..., :, None]
    dens_own = center[8][..., :, None]
    factor_own = center[9][..., :, None]
    sound_own = center[10][..., :, None]
    totals = [jnp.zeros(center.shape[1:], jnp.float32) for axis_id in range(3)]
    for shift in neighbour_shifts():
        neighbour = neighbour_cells(around, shift, center)
        parts = separation(center, neighbour, shift)
        radius_sq = parts[0] ** 2 + parts[1] ** 2 + parts[2] ** 2
        approach = parts[0] * (center[3][..., :, None] - neighbour[3][..., None, :])
        approach = approach + parts[1] * (center[4][..., :, None] - neighbour[4][..., None, :])
        approach = approach + parts[2] * (center[5][..., :, None] - neighbour[5][..., None, :])
        smooth_far = neighbour[6][..., None, :]
        value_own, slope_own = kernel_terms(radius_sq, smooth_own)
        value_far, slope_far = kernel_terms(radius_sq, smooth_far)
        mean_smooth = 0.5 * (smooth_own + smooth_far)
        closing = mean_smooth * jnp.minimum(approach, 0.0) / (radius_sq + 0.01 * mean_smooth ** 2)
        viscous = (-visc_alpha * 0.5 * (sound_own + neighbour[10][..., None, :]) * closing + visc_beta * closing ** 2) / (0.5 * (dens_own + neighbour[8][..., None, :]))
        weight = neighbour[7][..., None, :] * (factor_own * slope_own + neighbour[9][..., None, :] * slope_far + viscous * 0.5 * (slope_own + slope_far))
        for axis_id in range(3):
            totals[axis_id] = totals[axis_id] - lax.optimization_barrier(jnp.sum(weight * parts[axis_id], axis=-1))
    return jnp.stack(totals)

def reference(offsets, velocities, smoothing, mass, entropy, prior_density, active):
    fields = jnp.concatenate([offsets, velocities, smoothing[None], mass[None], entropy[None]], axis=0)
    pad_width = ((0, 0), (1, 1), (1, 1), (1, 1), (0, 0))
    padded = jnp.pad(fields, pad_width, mode='wrap')

    def density_slab(index):
        return density_block(lax.dynamic_slice_in_dim(padded, index, 3, 1))[0]
    computed = lax.map(density_slab, jnp.arange(NX, dtype=jnp.int32))
    live = active == 1
    density = jnp.where(live, computed, prior_density)
    factor = entropy * density ** (-1.0 / 3.0)
    sound = jnp.sqrt(5.0 / 3.0 * entropy * density ** (2.0 / 3.0))
    forces = jnp.concatenate([fields[:8], density[None], factor[None], sound[None]], axis=0)
    padded_force = jnp.pad(forces, pad_width, mode='wrap')

    def force_slab(index):
        return force_block(lax.dynamic_slice_in_dim(padded_force, index, 3, 1))[:, 0]
    accel = jnp.moveaxis(lax.map(force_slab, jnp.arange(NX, dtype=jnp.int32)), 0, 1)
    accel = jnp.where(live[None], accel, 0.0)
    return (density, accel)
```

```python
import functools
import math

import jax
import jax.numpy as jnp
from jax import lax
from jax.experimental import pallas as pl
from jax.experimental.pallas import tpu as pltpu
from jax.sharding import PartitionSpec as P

kernel_norm = 21.0 / (2.0 * math.pi)
visc_alpha = 1.0
visc_beta = 2.0

ROWS = 8
FEATS = 16
TINY = 1e-30
VMEM = pltpu.VMEM
F32 = jnp.float32
BF16 = jnp.bfloat16


def neighbour_shifts():
    return [
        (step_x, step_y, step_z)
        for step_x in (-1, 0, 1)
        for step_y in (-1, 0, 1)
        for step_z in (-1, 0, 1)
    ]


def split_parts(values):
    high = values.astype(BF16)
    rest = values - high.astype(F32)
    middle = rest.astype(BF16)
    low = (rest - middle.astype(F32)).astype(BF16)
    return (high, middle, low)


def exact_dot(left, right, dims):
    total = None
    for a in left:
        for b in right:
            part = lax.dot_general(a, b, (dims, ((), ())), preferred_element_type=F32)
            total = part if total is None else total + part
    return total


def pack_kernel(offsets, velocities, smoothing, mass, entropy, out, sems):
    pieces = [
        (offsets, out.at[0:3]),
        (velocities, out.at[3:6]),
        (smoothing, out.at[6]),
        (mass, out.at[7]),
        (entropy, out.at[8]),
    ]
    copies = [pltpu.make_async_copy(a, b, sems.at[k]) for k, (a, b) in enumerate(pieces)]
    for copy in copies:
        copy.start()
    for copy in copies:
        copy.wait()


def pack(offsets, velocities, smoothing, mass, entropy):
    anywhere = pl.BlockSpec(memory_space=pl.ANY)
    return pl.pallas_call(
        pack_kernel,
        out_shape=jax.ShapeDtypeStruct((9,) + smoothing.shape, F32),
        in_specs=[anywhere] * 5,
        out_specs=pl.BlockSpec(memory_space=VMEM),
        scratch_shapes=[pltpu.SemaphoreType.DMA((5,))],
        name="pack",
    )(offsets, velocities, smoothing, mass, entropy)


def active_ranks(live):
    size = live.shape[1]
    before = lax.broadcasted_iota(jnp.int32, (size, size), 0)
    after = lax.broadcasted_iota(jnp.int32, (size, size), 1)
    lower = jnp.where(before < after, 1.0, 0.0).astype(BF16)
    ranks = jnp.dot(live.astype(BF16), lower, preferred_element_type=F32)
    return jnp.where(live > 0.5, ranks, -1.0)


def selection(ranks_row, size):
    rank = lax.broadcasted_iota(jnp.int32, (size, size), 0).astype(F32)
    return jnp.where(rank == ranks_row, 1.0, 0.0).astype(BF16)


def grid_of(cells):
    nx, ny, nz = cells
    wide_y, wide_z = ny + 2, nz + 2
    return nx * ny * nz, (nx + 2) * wide_y * wide_z, wide_y * wide_z, wide_z


def wide_row(cell, cells):
    nx, ny, nz = cells
    _, _, step_x, step_y = grid_of(cells)
    a = cell // (ny * nz)
    b = (cell // nz) % ny
    c = cell % nz
    return (a + 1) * step_x + (b + 1) * step_y + c + 1


def cell_origin(count, cells):
    _, _, step_x, step_y = grid_of(cells)
    row = lax.broadcasted_iota(jnp.int32, (count, 128), 0)
    x = row // step_x
    y = (row // step_y) % (step_x // step_y)
    z = row % step_y
    return [part.astype(F32) - 2.0 for part in (x, y, z)]


def run_cells(cells, live_ref, feats_ref, rank_ref, ic_ref, res_ref, tile_body, finish):
    own, wide, step_x, step_y = grid_of(cells)
    size = live_ref.shape[1]
    rank_ref[...] = active_ranks(live_ref[...].astype(F32))

    def one_cell(cell, carry):
        ranks = rank_ref[pl.ds(cell, 1), :]
        base = wide_row(cell, cells)
        count = jnp.sum(jnp.where(ranks >= 0.0, 1, 0))
        select = selection(ranks, size)
        picked = feats_ref[pl.ds(base, FEATS, stride=wide), :]
        ic_ref[...] = exact_dot([select], split_parts(picked), ((1,), (1,)))
        res_ref[...] = jnp.zeros_like(res_ref)

        def one_tile(tile, inner):
            start = pl.multiple_of(tile * ROWS, ROWS)
            sums = tile_body(ic_ref[pl.ds(start, ROWS), :], base)
            lanes = lax.broadcasted_iota(jnp.int32, (ROWS, ROWS), 1)
            block = jnp.zeros((ROWS, ROWS), F32)
            for k, part in enumerate(sums):
                column = jnp.sum(part, axis=1, keepdims=True)
                block = jnp.where(lanes == k, column, block)
            res_ref[pl.ds(start, ROWS), :] = block
            return inner

        lax.fori_loop(0, (count + ROWS - 1) // ROWS, one_tile, 0)
        back = exact_dot(split_parts(res_ref[...].T), [select], ((1,), (0,)))
        finish(cell, ranks, back)
        return carry

    lax.fori_loop(0, own, one_cell, 0)


def density_kernel(cells, fields, live, prior, out, feats, rank, ic, res):
    own, wide, step_x, step_y = grid_of(cells)
    for k, origin in enumerate(cell_origin(wide, cells)):
        feats[k * wide : (k + 1) * wide, :] = fields[k * wide : (k + 1) * wide, :] + origin
    smooth = fields[6 * wide : 7 * wide, :]
    inverse = 1.0 / smooth
    feats[3 * wide : 4 * wide, :] = inverse * inverse
    feats[4 * wide : 5 * wide, :] = kernel_norm * inverse * inverse * inverse
    feats[5 * wide : 6 * wide, :] = fields[7 * wide : 8 * wide, :]
    feats[6 * wide :, :] = jnp.zeros(((FEATS - 6) * wide, 128), F32)

    def tile_body(tile, base):
        size = feats.shape[1]
        own_x, own_y, own_z, scale, norm = [
            jnp.broadcast_to(tile[:, k : k + 1], (ROWS, size)) for k in range(5)
        ]
        total = jnp.zeros((ROWS, size), F32)
        for shift in neighbour_shifts():
            row = base + (shift[0] * step_x + shift[1] * step_y + shift[2])
            far = [feats[pl.ds(row + k * wide, ROWS, stride=0), :] for k in (0, 1, 2, 5)]
            dx, dy, dz = own_x - far[0], own_y - far[1], own_z - far[2]
            square = (dx * dx + dy * dy + dz * dz) * scale
            ratio = square * lax.rsqrt(jnp.maximum(square, TINY))
            inside = jnp.maximum(1.0 - ratio, 0.0)
            second = inside * inside
            total = total + (second * second) * (5.0 - 4.0 * inside) * far[3]
        return [total * norm]

    def finish(cell, ranks, back):
        out[pl.ds(cell, 1), :] = jnp.where(ranks >= 0.0, back[0:1, :], prior[pl.ds(cell, 1), :])

    run_cells(cells, live, feats, rank, ic, res, tile_body, finish)


def force_kernel(cells, fields, density, live, out, feats, rank, ic, res):
    own, wide, step_x, step_y = grid_of(cells)

    def put(k, value):
        feats[k * wide : (k + 1) * wide, :] = value

    def get(k):
        return fields[k * wide : (k + 1) * wide, :]

    for k, origin in enumerate(cell_origin(wide, cells)):
        put(k, get(k) + origin)
        put(3 + k, get(3 + k))
    smooth = get(6)
    dens = density[...]
    entropy = get(8)
    log_dens = jnp.log(dens)
    peak = (20.0 * kernel_norm) ** (1.0 / 3.0) * jnp.exp(jnp.log(smooth) * (-5.0 / 3.0))
    put(6, peak)
    put(7, peak / smooth)
    put(8, 0.05 * smooth)
    put(9, entropy * jnp.exp(log_dens * (-1.0 / 3.0)))
    put(10, jnp.sqrt(5.0 / 3.0 * entropy * jnp.exp(log_dens * (2.0 / 3.0))) * (visc_alpha / 40.0))
    put(11, dens * (1.0 / 200.0))
    put(12, get(7))
    feats[13 * wide :, :] = jnp.zeros(((FEATS - 13) * wide, 128), F32)

    def tile_body(tile, base):
        size = feats.shape[1]
        mine = [jnp.broadcast_to(tile[:, k : k + 1], (ROWS, size)) for k in range(12)]
        totals = [jnp.zeros((ROWS, size), F32) for axis in range(3)]
        for shift in neighbour_shifts():
            row = base + (shift[0] * step_x + shift[1] * step_y + shift[2])
            far = [feats[pl.ds(row + k * wide, ROWS, stride=0), :] for k in range(13)]
            parts = [mine[k] - far[k] for k in range(3)]
            square = parts[0] * parts[0] + parts[1] * parts[1] + parts[2] * parts[2]
            approach = parts[0] * (mine[3] - far[3])
            approach = approach + parts[1] * (mine[4] - far[4])
            approach = approach + parts[2] * (mine[5] - far[5])
            radius = square * lax.rsqrt(jnp.maximum(square, TINY))
            slope_own = jnp.maximum(mine[6] - radius * mine[7], 0.0)
            slope_far = jnp.maximum(far[6] - radius * far[7], 0.0)
            slope_own = slope_own * slope_own * slope_own
            slope_far = slope_far * slope_far * slope_far
            reach = mine[8] + far[8]
            closing = jnp.minimum(approach, 0.0) * reach / (square + reach * reach)
            viscous = closing * (closing - (mine[10] + far[10])) / (mine[11] + far[11])
            weight = far[12] * (slope_own * (mine[9] + viscous) + slope_far * (far[9] + viscous))
            for axis in range(3):
                totals[axis] = totals[axis] + weight * parts[axis]
        return totals

    def finish(cell, ranks, back):
        for axis in range(3):
            out[pl.ds(axis * own + cell, 1), :] = back[axis : axis + 1, :]

    run_cells(cells, live, feats, rank, ic, res, tile_body, finish)


def pair_call(kernel, name, out_rows, cells, pairs_cost, *operands):
    own, wide, _, _ = grid_of(cells)
    size = operands[0].shape[-1]
    space = pl.BlockSpec(memory_space=VMEM)
    return pl.pallas_call(
        functools.partial(kernel, cells),
        out_shape=jax.ShapeDtypeStruct((out_rows, size), F32),
        in_specs=[space] * len(operands),
        out_specs=space,
        scratch_shapes=[
            VMEM((FEATS * wide, size), F32),
            VMEM((own, size), F32),
            VMEM((size, FEATS), F32),
            VMEM((size, ROWS), F32),
        ],
        name=name,
    )(*operands)


def ring(count, step):
    return [(i, (i + step) % count) for i in range(count)]


def extended(block, axis, dim):
    count = lax.axis_size(axis)
    length = block.shape[dim]
    head = lax.slice_in_dim(block, 0, 1, axis=dim)
    tail = lax.slice_in_dim(block, length - 1, length, axis=dim)
    if count == 2 and length <= 2:
        other = lax.ppermute(block, axis, ring(count, 1))
        below = lax.slice_in_dim(other, length - 1, length, axis=dim)
        above = lax.slice_in_dim(other, 0, 1, axis=dim)
    else:
        below = lax.ppermute(tail, axis, ring(count, 1))
        above = lax.ppermute(head, axis, ring(count, -1))
    return jnp.concatenate([below, block, above], axis=dim)


def ghost_cells(block):
    for axis, dim in (("gx", 1), ("gy", 2), ("gz", 3)):
        block = extended(block, axis, dim)
    return block


def body(offsets, velocities, smoothing, mass, entropy, prior_density, active):
    cells = smoothing.shape[:3]
    size = smoothing.shape[3]
    own, wide, _, _ = grid_of(cells)
    fields = ghost_cells(pack(offsets, velocities, smoothing, mass, entropy))
    fields = fields.reshape(9 * wide, size)
    live = active.reshape(own, size)
    prior = prior_density.reshape(own, size)
    density = pair_call(density_kernel, "density", own, cells, 20, fields, live, prior)
    density = density.reshape(cells + (size,))
    around = ghost_cells(density[None]).reshape(wide, size)
    accel = pair_call(force_kernel, "force", 3 * own, cells, 60, fields, around, live)
    return (density, accel.reshape((3,) + cells + (size,)))


def solution(mesh):
    grid = ("gx", "gy", "gz", None)
    in_specs = (P(None, *grid), P(None, *grid)) + (P(*grid),) * 5
    out_specs = (P(*grid), P(None, *grid))
    return jax.shard_map(body, mesh=mesh, in_specs=in_specs, out_specs=out_specs, check_vma=False)
```

```python
import functools
import math

import jax
import jax.numpy as jnp
from jax import lax
from jax.experimental import pallas as pl
from jax.experimental.pallas import tpu as pltpu
from jax.sharding import PartitionSpec as P

kernel_norm = 21.0 / (2.0 * math.pi)
visc_alpha = 1.0
visc_beta = 2.0

ROWS = 8
TINY = 1e-30
VMEM = pltpu.VMEM
F32 = jnp.float32
BF16 = jnp.bfloat16


def neighbour_shifts():
    return [
        (step_x, step_y, step_z)
        for step_x in (-1, 0, 1)
        for step_y in (-1, 0, 1)
        for step_z in (-1, 0, 1)
    ]


def pack_kernel(offsets, velocities, smoothing, mass, entropy, out, sems):
    pieces = [
        (offsets, out.at[0:3]),
        (velocities, out.at[3:6]),
        (smoothing, out.at[6]),
        (mass, out.at[7]),
        (entropy, out.at[8]),
    ]
    copies = [pltpu.make_async_copy(a, b, sems.at[k]) for k, (a, b) in enumerate(pieces)]
    for copy in copies:
        copy.start()
    for copy in copies:
        copy.wait()


def pack(offsets, velocities, smoothing, mass, entropy):
    anywhere = pl.BlockSpec(memory_space=pl.ANY)
    return pl.pallas_call(
        pack_kernel,
        out_shape=jax.ShapeDtypeStruct((9,) + smoothing.shape, F32),
        in_specs=[anywhere] * 5,
        out_specs=pl.BlockSpec(memory_space=VMEM),
        scratch_shapes=[pltpu.SemaphoreType.DMA((5,))],
        name="pack",
    )(offsets, velocities, smoothing, mass, entropy)


def active_ranks(live):
    size = live.shape[1]
    before = lax.broadcasted_iota(jnp.int32, (size, size), 0)
    after = lax.broadcasted_iota(jnp.int32, (size, size), 1)
    lower = jnp.where(before < after, 1.0, 0.0).astype(BF16)
    ranks = jnp.dot(live.astype(BF16), lower, preferred_element_type=F32)
    return jnp.where(live > 0.5, ranks, -1.0)


def grid_of(cells):
    nx, ny, nz = cells
    wide_y, wide_z = ny + 2, nz + 2
    return nx * ny * nz, (nx + 2) * wide_y * wide_z, wide_y * wide_z, wide_z


def wide_row(cell, cells):
    nx, ny, nz = cells
    _, _, step_x, step_y = grid_of(cells)
    a = cell // (ny * nz)
    b = (cell // nz) % ny
    c = cell % nz
    return (a + 1) * step_x + (b + 1) * step_y + c + 1


def cell_origin(count, cells):
    _, _, step_x, step_y = grid_of(cells)
    row = lax.broadcasted_iota(jnp.int32, (count, 128), 0)
    x = row // step_x
    y = (row // step_y) % (step_x // step_y)
    z = row % step_y
    return [part.astype(F32) - 2.0 for part in (x, y, z)]


def run_tiles(cells, used, sums, refs, pair_sums):
    live, feats, rank, mine, parts, back, table = refs
    own, wide, _, _ = grid_of(cells)
    size = live.shape[1]
    ranks = active_ranks(live[...].astype(F32))
    rank[...] = ranks
    counts = jnp.sum(jnp.where(ranks >= 0.0, 1, 0), axis=1, keepdims=True)
    parts[...] = jnp.zeros_like(parts)
    back[...] = jnp.zeros_like(back)

    total = jnp.int32(0)
    table[0] = 0
    for cell in range(own):
        tiles = (jnp.sum(counts[cell : cell + 1, :]) + ROWS - 1) // ROWS

        def note(tile, carry, cell=cell, total=total):
            table[total + tile] = cell * size + tile
            return carry

        lax.fori_loop(0, tiles, note, 0)
        total = total + tiles
    table[total] = 0
    lines = lax.broadcasted_iota(jnp.int32, (ROWS, size), 0)

    def place(turn):
        entry = table[turn]
        cell = entry // size
        first = (entry % size) * ROWS
        row = rank[pl.ds(cell, ROWS, stride=0), :]
        return cell, row == (lines + first).astype(F32)

    def gathered(turn):
        cell, hit = place(turn)
        base = wide_row(cell, cells)
        values = []
        for k in range(used):
            row = feats[pl.ds(k * wide + base, ROWS, stride=0), :]
            column = jnp.sum(jnp.where(hit, row, 0.0), axis=1, keepdims=True)
            values.append(jnp.broadcast_to(column, (ROWS, size)))
        return values

    def returned(turn, slot):
        cell, hit = place(turn)
        values = []
        for k in range(sums):
            part = parts[pl.ds(pl.multiple_of((slot * sums + k) * ROWS, ROWS), ROWS), :]
            column = jnp.sum(part, axis=1, keepdims=True)
            at = pl.ds(pl.multiple_of((k * own + cell) * ROWS, ROWS), ROWS)
            values.append((at, back[at, :] + jnp.where(hit, column, 0.0)))
        return values

    def keep(slot, values):
        for k, value in enumerate(values):
            mine[pl.ds(pl.multiple_of((slot * used + k) * ROWS, ROWS), ROWS), :] = value

    def turn_body(turn, carry):
        slot = turn % 2
        values = [
            mine[pl.ds(pl.multiple_of((slot * used + k) * ROWS, ROWS), ROWS), :]
            for k in range(used)
        ]
        later = gathered(turn + 1)
        earlier = returned(jnp.maximum(turn - 1, 0), 1 - slot)
        result = pair_sums(values, wide_row(table[turn] // size, cells))
        for at, value in earlier:
            back[at, :] = value
        keep(1 - slot, later)
        for k, value in enumerate(result):
            parts[pl.ds(pl.multiple_of((slot * sums + k) * ROWS, ROWS), ROWS), :] = value
        return carry

    keep(0, gathered(0))
    lax.fori_loop(0, total, turn_body, 0)

    @pl.when(total > 0)
    def _():
        for at, value in returned(total - 1, (total - 1) % 2):
            back[at, :] = value

    own_rows = []
    for k in range(sums * own):
        own_rows.append(jnp.sum(back[k * ROWS : (k + 1) * ROWS, :], axis=0, keepdims=True))
    return ranks, own_rows


DENSITY_USED, DENSITY_FEATS, DENSITY_SUMS = 4, 6, 1
FORCE_USED, FORCE_FEATS, FORCE_SUMS = 12, 13, 3


def density_kernel(cells, fields, live, prior, out, feats, *scratch):
    own, wide, step_x, step_y = grid_of(cells)

    def put(k, value):
        feats[k * wide : (k + 1) * wide, :] = value

    for k, origin in enumerate(cell_origin(wide, cells)):
        put(k, fields[k * wide : (k + 1) * wide, :] + origin)
    inverse = 1.0 / fields[6 * wide : 7 * wide, :]
    mass = fields[7 * wide : 8 * wide, :]
    put(3, inverse)
    put(4, 5.0 * mass)
    put(5, 4.0 * mass)

    def pair_sums(mine, base):
        scale = mine[3] * mine[3]
        total = jnp.zeros_like(scale)
        for shift in neighbour_shifts():
            row = base + (shift[0] * step_x + shift[1] * step_y + shift[2])
            far = [feats[pl.ds(row + k * wide, ROWS, stride=0), :] for k in (0, 1, 2, 4, 5)]
            dx, dy, dz = mine[0] - far[0], mine[1] - far[1], mine[2] - far[2]
            square = (dx * dx + dy * dy + dz * dz) * scale
            ratio = square * lax.rsqrt(jnp.maximum(square, TINY))
            inside = jnp.maximum(1.0 - ratio, 0.0)
            second = inside * inside
            total = total + (second * second) * (far[3] - far[4] * inside)
        return [total * (kernel_norm * mine[3] * scale)]

    refs = (live, feats) + scratch
    ranks, rows = run_tiles(cells, DENSITY_USED, DENSITY_SUMS, refs, pair_sums)
    for cell in range(own):
        at = slice(cell, cell + 1)
        out[at, :] = jnp.where(ranks[at, :] >= 0.0, rows[cell], prior[at, :])


def force_kernel(cells, fields, density, live, out, feats, *scratch):
    own, wide, step_x, step_y = grid_of(cells)

    def put(k, value):
        feats[k * wide : (k + 1) * wide, :] = value

    def get(k):
        return fields[k * wide : (k + 1) * wide, :]

    for k, origin in enumerate(cell_origin(wide, cells)):
        put(k, get(k) + origin)
        put(3 + k, get(3 + k))
    smooth = get(6)
    dens = density[...]
    entropy = get(8)
    log_dens = jnp.log(dens)
    peak = (20.0 * kernel_norm) ** (1.0 / 3.0) * jnp.exp(jnp.log(smooth) * (-5.0 / 3.0))
    put(6, peak)
    put(7, peak / smooth)
    put(8, 0.05 * smooth)
    put(9, entropy * jnp.exp(log_dens * (-1.0 / 3.0)))
    put(10, jnp.sqrt(5.0 / 3.0 * entropy * jnp.exp(log_dens * (2.0 / 3.0))) * (visc_alpha / 40.0))
    put(11, dens * (1.0 / 200.0))
    put(12, get(7))

    def pair_sums(mine, base):
        totals = [jnp.zeros_like(mine[0]) for axis in range(3)]
        for shift in neighbour_shifts():
            row = base + (shift[0] * step_x + shift[1] * step_y + shift[2])
            far = [feats[pl.ds(row + k * wide, ROWS, stride=0), :] for k in range(FORCE_FEATS)]
            parts = [mine[k] - far[k] for k in range(3)]
            square = parts[0] * parts[0] + parts[1] * parts[1] + parts[2] * parts[2]
            approach = parts[0] * (mine[3] - far[3])
            approach = approach + parts[1] * (mine[4] - far[4])
            approach = approach + parts[2] * (mine[5] - far[5])
            radius = square * lax.rsqrt(jnp.maximum(square, TINY))
            slope_own = jnp.maximum(mine[6] - radius * mine[7], 0.0)
            slope_far = jnp.maximum(far[6] - radius * far[7], 0.0)
            slope_own = slope_own * slope_own * slope_own
            slope_far = slope_far * slope_far * slope_far
            reach = mine[8] + far[8]
            closing = jnp.minimum(approach, 0.0) * reach / (square + reach * reach)
            viscous = closing * (closing - (mine[10] + far[10])) / (mine[11] + far[11])
            weight = far[12] * (slope_own * (mine[9] + viscous) + slope_far * (far[9] + viscous))
            for axis in range(3):
                totals[axis] = totals[axis] + weight * parts[axis]
        return totals

    refs = (live, feats) + scratch
    ranks, rows = run_tiles(cells, FORCE_USED, FORCE_SUMS, refs, pair_sums)
    for k, row in enumerate(rows):
        out[k : k + 1, :] = row


def pair_call(kernel, name, used, feats, sums, cells, *operands):
    own, wide, _, _ = grid_of(cells)
    size = operands[0].shape[-1]
    space = pl.BlockSpec(memory_space=VMEM)
    return pl.pallas_call(
        functools.partial(kernel, cells),
        out_shape=jax.ShapeDtypeStruct((sums * own, size), F32),
        in_specs=[space] * len(operands),
        out_specs=space,
        scratch_shapes=[
            VMEM((feats * wide, size), F32),
            VMEM((own, size), F32),
            VMEM((2 * used * ROWS, size), F32),
            VMEM((2 * sums * ROWS, size), F32),
            VMEM((sums * own * ROWS, size), F32),
            pltpu.SMEM((own * (size // ROWS) + 1,), jnp.int32),
        ],
        name=name,
    )(*operands)


def ring(count, step):
    return [(i, (i + step) % count) for i in range(count)]


def extended(block, axis, dim):
    count = lax.axis_size(axis)
    length = block.shape[dim]
    head = lax.slice_in_dim(block, 0, 1, axis=dim)
    tail = lax.slice_in_dim(block, length - 1, length, axis=dim)
    if count == 2 and length <= 2:
        other = lax.ppermute(block, axis, ring(count, 1))
        below = lax.slice_in_dim(other, length - 1, length, axis=dim)
        above = lax.slice_in_dim(other, 0, 1, axis=dim)
    else:
        below = lax.ppermute(tail, axis, ring(count, 1))
        above = lax.ppermute(head, axis, ring(count, -1))
    return jnp.concatenate([below, block, above], axis=dim)


def ghost_cells(block):
    for axis, dim in (("gx", 1), ("gy", 2), ("gz", 3)):
        block = extended(block, axis, dim)
    return block


def body(offsets, velocities, smoothing, mass, entropy, prior_density, active):
    cells = smoothing.shape[:3]
    size = smoothing.shape[3]
    own, wide, _, _ = grid_of(cells)
    fields = ghost_cells(pack(offsets, velocities, smoothing, mass, entropy))
    fields = fields.reshape(9 * wide, size)
    live = active.reshape(own, size)
    prior = prior_density.reshape(own, size)
    density = pair_call(
        density_kernel, "density", DENSITY_USED, DENSITY_FEATS, DENSITY_SUMS, cells, fields, live, prior
    )
    density = density.reshape(cells + (size,))
    around = ghost_cells(density[None]).reshape(wide, size)
    accel = pair_call(
        force_kernel, "force", FORCE_USED, FORCE_FEATS, FORCE_SUMS, cells, fields, around, live
    )
    return (density, accel.reshape((3,) + cells + (size,)))


def solution(mesh):
    grid = ("gx", "gy", "gz", None)
    in_specs = (P(None, *grid), P(None, *grid)) + (P(*grid),) * 5
    out_specs = (P(*grid), P(None, *grid))
    return jax.shard_map(body, mesh=mesh, in_specs=in_specs, out_specs=out_specs, check_vma=False)
```

```python
import functools
import math

import jax
import jax.numpy as jnp
from jax import lax
from jax.experimental import pallas as pl
from jax.experimental.pallas import tpu as pltpu
from jax.sharding import PartitionSpec as P

kernel_norm = 21.0 / (2.0 * math.pi)
visc_alpha = 1.0
visc_beta = 2.0

ROWS = 8
TINY = 1e-30
VMEM_BYTES = 4 << 20
VMEM = pltpu.VMEM
F32 = jnp.float32
BF16 = jnp.bfloat16


def neighbour_shifts():
    return [
        (step_x, step_y, step_z)
        for step_x in (-1, 0, 1)
        for step_y in (-1, 0, 1)
        for step_z in (-1, 0, 1)
    ]


def pack_kernel(offsets, velocities, smoothing, mass, entropy, prior, active, *refs):
    out, prior_out, active_out, sems = refs
    pieces = [
        (offsets, out.at[0:3]),
        (velocities, out.at[3:6]),
        (smoothing, out.at[6]),
        (mass, out.at[7]),
        (entropy, out.at[8]),
        (prior, prior_out),
        (active, active_out),
    ]
    copies = [pltpu.make_async_copy(a, b, sems.at[k]) for k, (a, b) in enumerate(pieces)]
    for copy in copies:
        copy.start()
    for copy in copies:
        copy.wait()


def pack(*arrays):
    anywhere = pl.BlockSpec(memory_space=pltpu.HBM)
    shape = arrays[2].shape
    return pl.pallas_call(
        pack_kernel,
        out_shape=[
            jax.ShapeDtypeStruct((9,) + shape, F32),
            jax.ShapeDtypeStruct(shape, F32),
            jax.ShapeDtypeStruct(shape, arrays[6].dtype),
        ],
        in_specs=[anywhere] * len(arrays),
        out_specs=[pl.BlockSpec(memory_space=VMEM)] * 3,
        scratch_shapes=[pltpu.SemaphoreType.DMA((len(arrays),))],
        compiler_params=pltpu.CompilerParams(vmem_limit_bytes=VMEM_BYTES),
        name="pack",
    )(*[pltpu.with_memory_space_constraint(x, pltpu.HBM) for x in arrays])


def active_ranks(live):
    size = live.shape[1]
    before = lax.broadcasted_iota(jnp.int32, (size, size), 0)
    after = lax.broadcasted_iota(jnp.int32, (size, size), 1)
    lower = jnp.where(before < after, 1.0, 0.0).astype(BF16)
    ranks = jnp.dot(live.astype(BF16), lower, preferred_element_type=F32)
    return jnp.where(live > 0.5, ranks, -1.0)


def grid_of(cells):
    nx, ny, nz = cells
    wide_y, wide_z = ny + 2, nz + 2
    return nx * ny * nz, (nx + 2) * wide_y * wide_z, wide_y * wide_z, wide_z


def wide_row(cell, cells):
    nx, ny, nz = cells
    _, _, step_x, step_y = grid_of(cells)
    a = cell // (ny * nz)
    b = (cell // nz) % ny
    c = cell % nz
    return (a + 1) * step_x + (b + 1) * step_y + c + 1


def cell_origin(count, cells):
    _, _, step_x, step_y = grid_of(cells)
    row = lax.broadcasted_iota(jnp.int32, (count, 128), 0)
    x = row // step_x
    y = (row // step_y) % (step_x // step_y)
    z = row % step_y
    return [part.astype(F32) - 2.0 for part in (x, y, z)]


def run_tiles(cells, used, sums, refs, pair_sums):
    live, feats, rank, mine, parts, back, table = refs
    own, wide, _, _ = grid_of(cells)
    size = live.shape[1]
    ranks = active_ranks(live[...].astype(F32))
    rank[...] = ranks
    counts = jnp.sum(jnp.where(ranks >= 0.0, 1, 0), axis=1, keepdims=True)
    parts[...] = jnp.zeros_like(parts)
    back[...] = jnp.zeros_like(back)

    def entry_of(turn):
        return table[3 * turn], table[3 * turn + 1], table[3 * turn + 2]

    def write(turn, cell, first, base):
        table[3 * turn] = cell
        table[3 * turn + 1] = first
        table[3 * turn + 2] = base

    total = jnp.int32(0)
    numbers = [counts[cell, 0] for cell in range(own)]
    for cell in range(own):
        tiles = (numbers[cell] + ROWS - 1) // ROWS

        def note(tile, carry, cell=cell, total=total):
            write(total + tile, cell, tile * ROWS, wide_row(cell, cells))
            return carry

        lax.fori_loop(0, tiles, note, 0)
        total = total + tiles
    idle = (0, 0, wide_row(0, cells))
    write(total, *idle)
    write(total + 1, *idle)
    lines = lax.broadcasted_iota(jnp.int32, (ROWS, size), 0)

    def hits(entry):
        row = rank[pl.ds(entry[0], ROWS, stride=0), :]
        return row == (lines + entry[1]).astype(F32)

    def gathered(entry):
        hit = hits(entry)
        base = entry[2]
        values = []
        for k in range(used):
            row = feats[pl.ds(k * wide + base, ROWS, stride=0), :]
            column = jnp.sum(jnp.where(hit, row, 0.0), axis=1, keepdims=True)
            values.append(jnp.broadcast_to(column, (ROWS, size)))
        return values

    def returned(entry, slot):
        hit = hits(entry)
        cell = entry[0]
        values = []
        for k in range(sums):
            part = parts[pl.ds(pl.multiple_of((slot * sums + k) * ROWS, ROWS), ROWS), :]
            column = jnp.sum(part, axis=1, keepdims=True)
            at = pl.ds(pl.multiple_of((k * own + cell) * ROWS, ROWS), ROWS)
            values.append((at, back[at, :] + jnp.where(hit, column, 0.0)))
        return values

    def keep(slot, values):
        for k, value in enumerate(values):
            mine[pl.ds(pl.multiple_of((slot * used + k) * ROWS, ROWS), ROWS), :] = value

    def turn_body(turn, entries):
        before, current, after = entries
        slot = turn & 1
        values = [
            mine[pl.ds(pl.multiple_of((slot * used + k) * ROWS, ROWS), ROWS), :]
            for k in range(used)
        ]
        later = gathered(after)
        earlier = returned(before, 1 - slot)
        result = pair_sums(values, current[2])
        for at, value in earlier:
            back[at, :] = value
        keep(1 - slot, later)
        for k, value in enumerate(result):
            parts[pl.ds(pl.multiple_of((slot * sums + k) * ROWS, ROWS), ROWS), :] = value
        return current, after, entry_of(turn + 2)

    opening = tuple(jnp.int32(part) for part in idle)
    keep(0, gathered(entry_of(0)))
    last = lax.fori_loop(0, total, turn_body, (opening, entry_of(0), entry_of(1)))[0]

    @pl.when(total > 0)
    def _():
        for at, value in returned(last, (total - 1) & 1):
            back[at, :] = value

    own_rows = []
    for k in range(sums * own):
        own_rows.append(jnp.sum(back[k * ROWS : (k + 1) * ROWS, :], axis=0, keepdims=True))
    return ranks, own_rows


DENSITY_USED, DENSITY_FEATS, DENSITY_SUMS = 4, 6, 1
FORCE_USED, FORCE_FEATS, FORCE_SUMS = 12, 13, 3


def density_kernel(cells, fields, live, prior, out, copy, feats, *scratch):
    own, wide, step_x, step_y = grid_of(cells)

    def put(k, value):
        feats[k * wide : (k + 1) * wide, :] = value

    for k, origin in enumerate(cell_origin(wide, cells)):
        put(k, fields[k * wide : (k + 1) * wide, :] + origin)
    inverse = 1.0 / fields[6 * wide : 7 * wide, :]
    mass = fields[7 * wide : 8 * wide, :]
    put(3, inverse)
    put(4, 5.0 * mass)
    put(5, 4.0 * mass)

    def pair_sums(mine, base):
        scale = mine[3] * mine[3]
        total = jnp.zeros_like(scale)
        for shift in neighbour_shifts():
            row = base + (shift[0] * step_x + shift[1] * step_y + shift[2])
            far = [feats[pl.ds(row + k * wide, ROWS, stride=0), :] for k in (0, 1, 2, 4, 5)]
            dx, dy, dz = mine[0] - far[0], mine[1] - far[1], mine[2] - far[2]
            square = (dx * dx + dy * dy + dz * dz) * scale
            ratio = square * lax.rsqrt(jnp.maximum(square, TINY))
            inside = jnp.maximum(1.0 - ratio, 0.0)
            second = inside * inside
            total = total + (second * second) * (far[3] - far[4] * inside)
        return [total * (kernel_norm * mine[3] * scale)]

    refs = (live, feats) + scratch
    ranks, rows = run_tiles(cells, DENSITY_USED, DENSITY_SUMS, refs, pair_sums)
    for cell in range(own):
        at = slice(cell, cell + 1)
        value = jnp.where(ranks[at, :] >= 0.0, rows[cell], prior[at, :])
        out[at, :] = value
        copy[at, :] = value


def force_kernel(cells, fields, density, live, out, feats, *scratch):
    own, wide, step_x, step_y = grid_of(cells)

    def put(k, value):
        feats[k * wide : (k + 1) * wide, :] = value

    def get(k):
        return fields[k * wide : (k + 1) * wide, :]

    for k, origin in enumerate(cell_origin(wide, cells)):
        put(k, get(k) + origin)
        put(3 + k, get(3 + k))
    smooth = get(6)
    dens = density[...]
    entropy = get(8)
    log_dens = jnp.log(dens)
    peak = (20.0 * kernel_norm) ** (1.0 / 3.0) * jnp.exp(jnp.log(smooth) * (-5.0 / 3.0))
    put(6, peak)
    put(7, peak / smooth)
    put(8, 0.05 * smooth)
    put(9, entropy * jnp.exp(log_dens * (-1.0 / 3.0)))
    put(10, jnp.sqrt(5.0 / 3.0 * entropy * jnp.exp(log_dens * (2.0 / 3.0))) * (visc_alpha / 40.0))
    put(11, dens * (1.0 / 200.0))
    put(12, get(7))

    def pair_sums(mine, base):
        totals = [jnp.zeros_like(mine[0]) for axis in range(3)]
        for shift in neighbour_shifts():
            row = base + (shift[0] * step_x + shift[1] * step_y + shift[2])
            far = [feats[pl.ds(row + k * wide, ROWS, stride=0), :] for k in range(FORCE_FEATS)]
            parts = [mine[k] - far[k] for k in range(3)]
            square = parts[0] * parts[0] + parts[1] * parts[1] + parts[2] * parts[2]
            approach = parts[0] * (mine[3] - far[3])
            approach = approach + parts[1] * (mine[4] - far[4])
            approach = approach + parts[2] * (mine[5] - far[5])
            radius = square * lax.rsqrt(jnp.maximum(square, TINY))
            slope_own = jnp.maximum(mine[6] - radius * mine[7], 0.0)
            slope_far = jnp.maximum(far[6] - radius * far[7], 0.0)
            slope_own = slope_own * slope_own * slope_own
            slope_far = slope_far * slope_far * slope_far
            reach = mine[8] + far[8]
            closing = jnp.minimum(approach, 0.0) * reach / (square + reach * reach)
            viscous = closing * (closing - (mine[10] + far[10])) / (mine[11] + far[11])
            weight = far[12] * (slope_own * (mine[9] + viscous) + slope_far * (far[9] + viscous))
            for axis in range(3):
                totals[axis] = totals[axis] + weight * parts[axis]
        return totals

    refs = (live, feats) + scratch
    ranks, rows = run_tiles(cells, FORCE_USED, FORCE_SUMS, refs, pair_sums)
    for k, row in enumerate(rows):
        out[k : k + 1, :] = row


def pair_call(kernel, name, outs, used, feats, sums, cells, *operands):
    own, wide, _, _ = grid_of(cells)
    size = operands[0].shape[-1]
    space = pl.BlockSpec(memory_space=VMEM)
    return pl.pallas_call(
        functools.partial(kernel, cells),
        out_shape=[jax.ShapeDtypeStruct((sums * own, size), F32)] * outs,
        in_specs=[space] * len(operands),
        out_specs=[space] * outs,
        scratch_shapes=[
            VMEM((feats * wide, size), F32),
            VMEM((own, size), F32),
            VMEM((2 * used * ROWS, size), F32),
            VMEM((2 * sums * ROWS, size), F32),
            VMEM((sums * own * ROWS, size), F32),
            pltpu.SMEM((3 * (own * (size // ROWS) + 2),), jnp.int32),
        ],
        compiler_params=pltpu.CompilerParams(vmem_limit_bytes=VMEM_BYTES),
        name=name,
    )(*operands)


def ring(count, step):
    return [(i, (i + step) % count) for i in range(count)]


def extended(block, axis, dim):
    count = lax.axis_size(axis)
    length = block.shape[dim]
    head = lax.slice_in_dim(block, 0, 1, axis=dim)
    tail = lax.slice_in_dim(block, length - 1, length, axis=dim)
    if count == 2 and length <= 2:
        other = lax.ppermute(block, axis, ring(count, 1))
        below = lax.slice_in_dim(other, length - 1, length, axis=dim)
        above = lax.slice_in_dim(other, 0, 1, axis=dim)
    else:
        below = lax.ppermute(tail, axis, ring(count, 1))
        above = lax.ppermute(head, axis, ring(count, -1))
    return jnp.concatenate([below, block, above], axis=dim)


def ghost_cells(block):
    for axis, dim in (("gx", 1), ("gy", 2), ("gz", 3)):
        block = extended(block, axis, dim)
    return block


def body(offsets, velocities, smoothing, mass, entropy, prior_density, active):
    cells = smoothing.shape[:3]
    size = smoothing.shape[3]
    own, wide, _, _ = grid_of(cells)
    fields, prior, live = pack(
        offsets, velocities, smoothing, mass, entropy, prior_density, active
    )
    fields = ghost_cells(fields).reshape(9 * wide, size)
    live = live.reshape(own, size)
    prior = prior.reshape(own, size)
    density, shared = pair_call(
        density_kernel,
        "density",
        2,
        DENSITY_USED,
        DENSITY_FEATS,
        DENSITY_SUMS,
        cells,
        *(fields, live, prior),
    )
    density = density.reshape(cells + (size,))
    around = ghost_cells(shared.reshape((1,) + cells + (size,))).reshape(wide, size)
    (accel,) = pair_call(
        force_kernel,
        "force",
        1,
        FORCE_USED,
        FORCE_FEATS,
        FORCE_SUMS,
        cells,
        *(fields, around, live),
    )
    return (density, accel.reshape((3,) + cells + (size,)))


def solution(mesh):
    grid = ("gx", "gy", "gz", None)
    in_specs = (P(None, *grid), P(None, *grid)) + (P(*grid),) * 5
    out_specs = (P(*grid), P(None, *grid))
    return jax.shard_map(body, mesh=mesh, in_specs=in_specs, out_specs=out_specs, check_vma=False)
```
